256 devices in a mesh: ta: 4 (over z_lo, core), pa: 64 (over x, y, z_hi).
Axes of the slice: x: 4, y: 4, z: 8 (z_hi: 4, z_lo: 2; z = z_hi * 2 + z_lo), core: 2. Of those that a mesh axis runs over, the one named last changes fastest.
Arguments:
- green_freq: bfloat16 [256, 4, 256, 256], P('ta', None, 'pa'), may hold values from -6 to 6
- colloc: bfloat16 [4, 256, 1024], P(None, None, 'pa'), may hold values from -0.375 to 0.375
- core: bfloat16 [1024, 1024], replicated, may hold values from -0.1875 to 0.1875
Outputs:
- sigma_freq: bfloat16 [256, 4, 256, 256], P('ta', None, 'pa')
The draws below stay inside these ranges and needn't reach their ends.
All inputs are finite; a program needn't handle non-finite values.
Results may differ from the reference program's by a relative error of at most 0.03.
Values may be sent and summed in bfloat16 or wider, within the bound.
No kernel may reach another device: no remote copies, remote signals or barrier semaphores. Data moves between devices by JAX's collectives and lax.ppermute only.
A program may use at most 128 MiB of HBM per device.

```python
import jax
import jax.numpy as jnp
from jax import lax

NORB = 256
NPTS = 1024
NFREQ = 128
NTIME = 128
KPTS = 4


def block_levels(key, dims, pieces, least, largest):
    factor_of, own = 1.0, jax.random.fold_in(key, 6)
    for axis_at, blocks in pieces:
        steps = jnp.exp(jax.random.uniform(jax.random.fold_in(own, axis_at), (blocks,), jnp.float32, least / len(pieces), largest / len(pieces)))
        factor_of = factor_of * jnp.repeat(steps, dims[axis_at] // blocks).reshape([-1 if axis == axis_at else 1 for axis in range(len(dims))])
    return factor_of


def bell_draw(key, shape, width, reach, shards=(), kind=jnp.bfloat16):
    array = jax.random.normal(key, shape, jnp.float32) * width
    if len(shards) > 0:
        array = block_levels(key, shape, shards, -0.22, 0.18) * array
    return jnp.clip(array, min=-reach, max=reach).astype(kind)


def setup_inputs(seed: int = 0) -> dict:
    arg_keys = jax.random.split(jax.random.key(seed), 4)
    green_freq = bell_draw(arg_keys[0], (2 * NFREQ, KPTS, NORB, NORB), 1.0, 6.0, ((0, 4), (2, 64)))
    colloc = bell_draw(arg_keys[1], (KPTS, NORB, NPTS), NORB ** -0.5, 0.375, ((2, 64),))
    core = bell_draw(arg_keys[2], (NPTS, NPTS), NPTS ** -0.5, 0.1875)
    return dict(green_freq=green_freq, colloc=colloc, core=core)


def time_tables(nfreq, ntime):
    freq = jnp.arange(nfreq, dtype=jnp.float32)
    times = jnp.arange(ntime, dtype=jnp.float32)
    phase = jnp.pi * (2.0 * freq[None, :] + 1.0) * (times[:, None] + 0.5) / ntime
    cosine = jnp.cos(phase)
    sine = jnp.sin(phase)
    scale_fwd = 1.0 / jnp.sqrt(jnp.float32(nfreq))
    scale_back = 1.0 / jnp.sqrt(jnp.float32(ntime))
    plus = jnp.concatenate([cosine, sine], axis=1) * scale_fwd
    minus = jnp.concatenate([-cosine, sine], axis=1) * scale_fwd
    fwd = jnp.stack([plus, minus], axis=0)
    back = jnp.concatenate([cosine.T, sine.T], axis=0) * scale_back
    return (fwd, back)

def reference(green_freq, colloc, core):
    fwd, back = time_tables(NFREQ, NTIME)
    green_wide = green_freq.astype(jnp.float32)
    colloc_wide = colloc.astype(jnp.float32)

    def one_time(index):
        row = fwd[:, index, :]
        green = jnp.einsum('sw,wkij->skij', row, green_wide, precision=lax.Precision.HIGHEST).astype(jnp.bfloat16)
        half = jnp.einsum('skij,kjq->skiq', green.astype(jnp.float32), colloc_wide).astype(jnp.bfloat16)
        green_pts = jnp.einsum('kip,skiq->skpq', colloc_wide, half.astype(jnp.float32))
        bubble = (lax.optimization_barrier(jnp.sum(green_pts[0] * green_pts[1], axis=0)) / KPTS).astype(jnp.bfloat16)
        mixed = jnp.dot(core, bubble, preferred_element_type=jnp.float32).astype(jnp.bfloat16)
        screened = jnp.dot(mixed, core, preferred_element_type=jnp.float32).astype(jnp.bfloat16)
        source = (-green_pts[0] * screened.astype(jnp.float32)[None]).astype(jnp.bfloat16)
        outer = jnp.einsum('kip,kpq->kiq', colloc_wide, source.astype(jnp.float32)).astype(jnp.bfloat16)
        return jnp.einsum('kiq,kjq->kij', outer.astype(jnp.float32), colloc_wide).astype(jnp.bfloat16)
    sigma_time = lax.map(one_time, jnp.arange(NTIME, dtype=jnp.int32))
    result = jnp.einsum('wt,tkij->wkij', back, sigma_time.astype(jnp.float32), precision=lax.Precision.HIGHEST)
    return result.astype(jnp.bfloat16)
```

```python
import functools

import jax
import jax.numpy as jnp
from jax import lax
from jax.experimental import pallas as pl
from jax.experimental.pallas import tpu as pltpu
from jax.sharding import PartitionSpec as P

NFREQ = 128
NPTS = 1024
NORB = 256
bf16 = jnp.bfloat16
f32 = jnp.float32

CORE_SWAP = [(0, 1), (1, 0), (2, 3), (3, 2)]
CHIP_SWAP = [(0, 2), (2, 0), (1, 3), (3, 1)]
NT = ((1,), (1,))
TN = ((0,), (0,))


def x_shift(step):
    return [(i, (i + 16 * step) % 64) for i in range(64)]


def half_tables():
    freq = jnp.arange(NFREQ, dtype=f32)
    times = jnp.arange(NFREQ // 2, dtype=f32)
    phase = jnp.pi * (2.0 * freq[None, :] + 1.0) * (times[:, None] + 0.5) / NFREQ
    scale = 1.0 / jnp.sqrt(f32(NFREQ))
    return jnp.cos(phase) * scale, jnp.sin(phase) * scale


def dot(a, b, dims=((1,), (0,))):
    return lax.dot_general(a, b, (dims, ((), ())), preferred_element_type=f32)


def pair_kernel(TP, TQ, TW, x_ref, g_ref, core_ref, out_ref, t_ref, bub_ref, mix_ref, own_ref, tmp_ref):
    def p_step(pb, _):
        rows = pl.ds(pl.multiple_of(pb * TP, TP), TP)
        for k in range(4):
            xk = x_ref[k, rows, :]
            for s in range(2):
                t_ref[s * 4 + k] = dot(xk, g_ref[s, k]).astype(bf16)

        def q_step(qb, _):
            cols = pl.ds(pl.multiple_of(qb * TQ, TQ), TQ)
            acc = None
            for k in range(4):
                xq = x_ref[k, cols, :]
                v = dot(t_ref[k], xq, NT)
                if k < 2:
                    own_ref[k, rows, cols] = v
                w = dot(t_ref[4 + k], xq, NT)
                term = v * v - w * w
                acc = term if acc is None else acc + term
            bub_ref[rows, cols] = (acc * 0.25).astype(bf16)
            return 0

        lax.fori_loop(0, NPTS // TQ, q_step, 0)
        return 0

    lax.fori_loop(0, NPTS // TP, p_step, 0)

    def mixed_step(i, _):
        rows = pl.ds(pl.multiple_of(i * TW, TW), TW)
        mix_ref[rows, :] = dot(core_ref[rows, :], bub_ref[...]).astype(bf16)
        return 0

    lax.fori_loop(0, NPTS // TW, mixed_step, 0)

    def source_step(i, _):
        rows = pl.ds(pl.multiple_of(i * TW, TW), TW)
        w = dot(mix_ref[rows, :], core_ref[...])
        for k in range(2):
            source = (own_ref[k, rows, :] * w).astype(bf16)
            tmp_ref[k, rows, :] = dot(source, x_ref[k]).astype(bf16)
        return 0

    lax.fori_loop(0, NPTS // TW, source_step, 0)
    for k in range(2):
        out_ref[k] = dot(x_ref[k], tmp_ref[k], TN).astype(bf16)


def pair_call(x, g, core, TP=1024, TQ=256, TW=512):
    vm = pl.BlockSpec(memory_space=pltpu.VMEM)
    return pl.pallas_call(
        functools.partial(pair_kernel, TP, TQ, TW),
        out_shape=jax.ShapeDtypeStruct((2, NORB, NORB), bf16),
        in_specs=[vm] * 3,
        out_specs=vm,
        scratch_shapes=[
            pltpu.VMEM((8, TP, NORB), bf16),
            pltpu.VMEM((NPTS, NPTS), bf16),
            pltpu.VMEM((NPTS, NPTS), bf16),
            pltpu.VMEM((2, NPTS, NPTS), f32),
            pltpu.VMEM((2, NPTS, NORB), bf16),
        ],
        compiler_params=pltpu.CompilerParams(vmem_limit_bytes=48 << 20),
        cost_estimate=pl.CostEstimate(flops=11_000_000_000, bytes_accessed=6 << 20, transcendentals=0),
    )(x, g, core)


def local(green_freq, colloc, core):
    ta = lax.axis_index("ta")
    c = ta % 2
    xpos = lax.axis_index("pa") // 16
    cosine, sine = half_tables()
    table = jnp.where(ta < 2, cosine, sine)
    own_w = lax.dynamic_slice_in_dim(table, c * 64, 64, 1)
    other_w = lax.dynamic_slice_in_dim(table, 64 - c * 64, 64, 1)

    gf = green_freq.reshape(64, 2, 8, NORB)
    mine = lax.dynamic_index_in_dim(gf, c, 1, keepdims=False)
    theirs = lax.dynamic_index_in_dim(gf, 1 - c, 1, keepdims=False)
    arrived = lax.ppermute(theirs, "ta", CORE_SWAP)
    part = jnp.einsum("uw,wrj->urj", own_w, mine.astype(f32), precision=lax.Precision.HIGHEST)
    part += jnp.einsum("uw,wrj->urj", other_w, arrived.astype(f32), precision=lax.Precision.HIGHEST)
    part = part.astype(bf16)

    xt = jnp.swapaxes(colloc, 1, 2).reshape(2, 4, 8, NORB)
    xt = lax.dynamic_index_in_dim(xt, c, 0, keepdims=False)
    xmsg = jnp.broadcast_to(xt[:, None], (4, 16, 8, NORB)).reshape(64, 8, NORB)
    got = lax.all_to_all(jnp.concatenate([part, xmsg], 1), "pa", 0, 0, tiled=True)
    green = got[:, :8].reshape(64, 2, 4, NORB).swapaxes(0, 1).reshape(2, NORB, NORB)
    xpart = got[:, 8:]

    other = lax.ppermute(green, "ta", CHIP_SWAP)
    pieces = [xpart] + [lax.ppermute(xpart, "pa", x_shift(s)) for s in (1, 2, 3)]
    blocks = jnp.zeros((4, 64, 8, NORB), bf16)
    for s in range(4):
        blocks = lax.dynamic_update_slice_in_dim(blocks, pieces[s][None], (xpos - s) % 4, 0)
    xown = blocks.reshape(2, 2, 64, 8, NORB).swapaxes(1, 2).reshape(2, NPTS, NORB)

    gown = jnp.stack([green, other])
    gnext = lax.ppermute(gown, "ta", CORE_SWAP)
    xnext = lax.ppermute(xown, "ta", CORE_SWAP)
    out = pair_call(jnp.concatenate([xown, xnext], 0), jnp.concatenate([gown, gnext], 1), core)

    msg = out.reshape(2, 64, 4, NORB).swapaxes(0, 1).reshape(64, 8, NORB)
    back = lax.all_to_all(msg, "pa", 0, 0, tiled=True)
    back_next = lax.ppermute(back, "ta", CORE_SWAP)
    first = jnp.where(c == 0, back, back_next)
    second = jnp.where(c == 0, back_next, back)
    both = jnp.concatenate([first, second], 1)
    final = own_w * jnp.where(ta < 2, 2.0, -2.0)
    result = jnp.einsum("uw,urj->wrj", final, both.astype(f32), precision=lax.Precision.HIGHEST)
    return result.astype(bf16).reshape(64, 4, 4, NORB)


def solution(mesh):
    return jax.shard_map(
        local,
        mesh=mesh,
        in_specs=(P("ta", None, "pa", None), P(None, None, "pa"), P()),
        out_specs=P("ta", None, "pa", None),
        check_vma=False,
    )
```

```python
import functools

import jax
import jax.numpy as jnp
from jax import lax
from jax.experimental import pallas as pl
from jax.experimental.pallas import tpu as pltpu
from jax.sharding import PartitionSpec as P


NFREQ = 128
NPTS = 1024
NORB = 256
bf16 = jnp.bfloat16
f32 = jnp.float32

CORE_SWAP = [(0, 1), (1, 0), (2, 3), (3, 2)]
CHIP_SWAP = [(0, 2), (2, 0), (1, 3), (3, 1)]
NT = ((1,), (1,))
TN = ((0,), (0,))


def square_pairs(step):
    def partner(v, core):
        return v ^ 1 if core == 0 else ((v + 1) ^ 1) - 1 & 3

    pairs = []
    for ta in range(4):
        for i in range(64):
            x, y, z = i // 16, (i // 4) % 4, i % 4
            x = partner(x, ta % 2) if step & 2 else x
            y = partner(y, ta % 2) if step & 1 else y
            pairs.append((ta * 64 + i, ta * 64 + x * 16 + y * 4 + z))
    return pairs


def half_tables():
    freq = jnp.arange(NFREQ, dtype=f32)
    times = jnp.arange(NFREQ // 2, dtype=f32)
    phase = jnp.pi * (2.0 * freq[None, :] + 1.0) * (times[:, None] + 0.5) / NFREQ
    scale = 1.0 / jnp.sqrt(f32(NFREQ))
    return jnp.cos(phase) * scale, jnp.sin(phase) * scale


def dot(a, b, dims=((1,), (0,))):
    return lax.dot_general(a, b, (dims, ((), ())), preferred_element_type=f32)


def points_of(x_ref, slots, kk, rows):
    return jnp.concatenate([x_ref[slots[2 * kk], rows, :], x_ref[slots[2 * kk + 1], rows, :]], axis=1)


def half_bubble(TQ, slots, x_ref, g_mine, g_else, t_ref, own_ref, emit):
    every = pl.ds(0, NPTS)
    for kk in range(2):
        xk = points_of(x_ref, slots, kk, every)
        t_ref[kk] = dot(xk, g_mine[kk]).astype(bf16)
        t_ref[2 + kk] = dot(xk, g_else[kk]).astype(bf16)

    def q_step(qb, _):
        cols = pl.ds(pl.multiple_of(qb * TQ, TQ), TQ)
        acc = None
        for kk in range(2):
            xq = points_of(x_ref, slots, kk, cols)
            v = dot(t_ref[kk], xq, NT)
            if own_ref is not None:
                own_ref[kk, :, cols] = v
            w = dot(t_ref[2 + kk], xq, NT)
            term = v * v - w * w
            acc = term if acc is None else acc + term
        emit(cols, acc)
        return 0

    lax.fori_loop(0, NPTS // TQ, q_step, 0)


def first_kernel(TQ, slot_ref, x_ref, g_mine, g_else, acc_ref, own_ref, t_ref):
    slots = [slot_ref[i] for i in range(4)]

    def emit(cols, acc):
        acc_ref[:, cols] = acc

    half_bubble(TQ, slots, x_ref, g_mine, g_else, t_ref, own_ref, emit)


def second_kernel(TQ, TW, slot_ref, x_own, x_next, g_mine, g_else, acc_ref, own_ref, core_ref, out_ref,
                  t_ref, bub_ref, mix_ref, tmp_ref):
    slots = [slot_ref[i] for i in range(4)]

    def emit(cols, acc):
        bub_ref[:, cols] = ((acc + acc_ref[:, cols]) * 0.25).astype(bf16)

    half_bubble(TQ, slots, x_next, g_mine, g_else, t_ref, None, emit)

    def mixed_step(i, _):
        rows = pl.ds(pl.multiple_of(i * TW, TW), TW)
        mix_ref[rows, :] = dot(core_ref[rows, :], bub_ref[...]).astype(bf16)
        return 0

    lax.fori_loop(0, NPTS // TW, mixed_step, 0)
    every = pl.ds(0, NPTS)

    def source_step(i, _):
        rows = pl.ds(pl.multiple_of(i * TW, TW), TW)
        w = dot(mix_ref[rows, :], core_ref[...])
        for kk in range(2):
            source = (own_ref[kk, rows, :] * w).astype(bf16)
            tmp_ref[kk, rows, :] = dot(source, points_of(x_own, slots, kk, every)).astype(bf16)
        return 0

    lax.fori_loop(0, NPTS // TW, source_step, 0)
    for kk in range(2):
        out_ref[kk] = dot(points_of(x_own, slots, kk, every), tmp_ref[kk], TN).astype(bf16)


VM = pl.BlockSpec(memory_space=pltpu.VMEM)
SM = pl.BlockSpec(memory_space=pltpu.SMEM)


def first_call(slots, x, g_mine, g_else, TQ=256):
    return pl.pallas_call(
        functools.partial(first_kernel, TQ),
        out_shape=(
            jax.ShapeDtypeStruct((NPTS, NPTS), f32),
            jax.ShapeDtypeStruct((2, NPTS, NPTS), f32),
        ),
        in_specs=[SM] + [VM] * 3,
        out_specs=(VM, VM),
        scratch_shapes=[pltpu.VMEM((4, NPTS, NORB), bf16)],
        compiler_params=pltpu.CompilerParams(vmem_limit_bytes=20 << 20),
        cost_estimate=pl.CostEstimate(flops=2_700_000_000, bytes_accessed=2 << 20, transcendentals=0),
    )(slots, x, g_mine, g_else)


def second_call(slots, x_own, x_next, g_mine, g_else, acc, own, core, TQ=256, TW=512):
    return pl.pallas_call(
        functools.partial(second_kernel, TQ, TW),
        out_shape=jax.ShapeDtypeStruct((2, NORB, NORB), bf16),
        in_specs=[SM] + [VM] * 7,
        out_specs=VM,
        scratch_shapes=[
            pltpu.VMEM((4, NPTS, NORB), bf16),
            pltpu.VMEM((NPTS, NPTS), bf16),
            pltpu.VMEM((NPTS, NPTS), bf16),
            pltpu.VMEM((2, NPTS, NORB), bf16),
        ],
        compiler_params=pltpu.CompilerParams(vmem_limit_bytes=32 << 20),
        cost_estimate=pl.CostEstimate(flops=8_300_000_000, bytes_accessed=4 << 20, transcendentals=0),
    )(slots, x_own, x_next, g_mine, g_else, acc, own, core)


def to_green(rows):
    parts = rows.reshape(64, 2, 2, 4, 128)
    return jnp.transpose(parts, (2, 0, 3, 1, 4)).reshape(2, NORB, NORB)


def local(green_freq, colloc, core):
    ta = lax.axis_index("ta")
    c = ta % 2
    pa = lax.axis_index("pa")
    xpos, ypos = pa // 16, (pa // 4) % 4
    cosine, sine = half_tables()
    table = jnp.where(ta < 2, cosine, sine)
    own_w = lax.dynamic_slice_in_dim(table, c * 64, 64, 1)
    other_w = lax.dynamic_slice_in_dim(table, 64 - c * 64, 64, 1)

    gf = green_freq.reshape(64, 2, 8, NORB)
    mine = lax.dynamic_index_in_dim(gf, c, 1, keepdims=False)
    theirs = lax.dynamic_index_in_dim(gf, 1 - c, 1, keepdims=False)
    arrived = lax.ppermute(theirs, "ta", CORE_SWAP)
    part = jnp.einsum("uw,wrj->urj", own_w, mine.astype(f32), precision=lax.Precision.HIGHEST)
    part += jnp.einsum("uw,wrj->urj", other_w, arrived.astype(f32), precision=lax.Precision.HIGHEST)
    part = part.astype(bf16).reshape(64, 8, 2, 128).swapaxes(1, 2).reshape(64, 16, 128)

    xt = jnp.swapaxes(colloc, 1, 2).reshape(2, 2, 16, 2, 128)
    xt = lax.dynamic_index_in_dim(xt, c, 0, keepdims=False).swapaxes(1, 2).reshape(4, 16, 128)
    xmsg = jnp.broadcast_to(xt.reshape(1, 2, 1, 2, 1, 16, 128), (2, 2, 2, 2, 4, 16, 128)).reshape(64, 16, 128)
    got = lax.all_to_all(jnp.concatenate([part, xmsg], 1), "pa", 0, 0, tiled=True)
    g_own = to_green(got[:, :16])
    xpart = got[:, 16:].reshape(NPTS, 128)

    g_kind = lax.ppermute(g_own, "ta", CHIP_SWAP)
    pieces = [xpart]
    for s in (1, 2, 3):
        pieces.append(lax.ppermute(xpart, ("ta", "pa"), square_pairs(s)))
    g_next = lax.ppermute(g_own, "ta", CORE_SWAP)
    x_own = jnp.stack(pieces)
    x_next = lax.ppermute(x_own, "ta", CORE_SWAP)
    g_last = lax.ppermute(g_kind, "ta", CORE_SWAP)
    here = 2 * (xpos % 2) + ypos % 2
    slots = jnp.arange(4, dtype=jnp.int32) ^ here
    acc, own = first_call(slots, x_own, g_own, g_kind)
    out = second_call(slots, x_own, x_next, g_next, g_last, acc, own, core)

    msg = out.reshape(2, 64, 4, NORB).swapaxes(0, 1).reshape(64, 8, NORB)
    back = lax.all_to_all(msg, "pa", 0, 0, tiled=True)
    back_next = lax.ppermute(back, "ta", CORE_SWAP)
    first = jnp.where(c == 0, back, back_next)
    second = jnp.where(c == 0, back_next, back)
    both = jnp.concatenate([first, second], 1)
    final = own_w * jnp.where(ta < 2, 2.0, -2.0)
    result = jnp.einsum("uw,urj->wrj", final, both.astype(f32), precision=lax.Precision.HIGHEST)
    return result.astype(bf16).reshape(64, 4, 4, NORB)


def solution(mesh):
    return jax.shard_map(
        local,
        mesh=mesh,
        in_specs=(P("ta", None, "pa", None), P(None, None, "pa"), P()),
        out_specs=P("ta", None, "pa", None),
        check_vma=False,
    )
```

```python
import functools

import jax
import jax.numpy as jnp
from jax import lax
from jax.experimental import pallas as pl
from jax.experimental.pallas import tpu as pltpu
from jax.sharding import PartitionSpec as P


NFREQ = 128
NPTS = 1024
NORB = 256
bf16 = jnp.bfloat16
f32 = jnp.float32

CORE_SWAP = [(0, 1), (1, 0), (2, 3), (3, 2)]
CHIP_SWAP = [(0, 2), (2, 0), (1, 3), (3, 1)]
NT = ((1,), (1,))
TN = ((0,), (0,))


def square_pairs(step):
    def partner(v, core):
        return v ^ 1 if core == 0 else ((v + 1) ^ 1) - 1 & 3

    pairs = []
    for ta in range(4):
        for i in range(64):
            x, y, z = i // 16, (i // 4) % 4, i % 4
            x = partner(x, ta % 2) if step & 2 else x
            y = partner(y, ta % 2) if step & 1 else y
            pairs.append((ta * 64 + i, ta * 64 + x * 16 + y * 4 + z))
    return pairs


def half_tables():
    freq = jnp.arange(NFREQ, dtype=f32)
    times = jnp.arange(NFREQ // 2, dtype=f32)
    phase = jnp.pi * (2.0 * freq[None, :] + 1.0) * (times[:, None] + 0.5) / NFREQ
    scale = 1.0 / jnp.sqrt(f32(NFREQ))
    return jnp.cos(phase) * scale, jnp.sin(phase) * scale


def dot(a, b, dims=((1,), (0,))):
    return lax.dot_general(a, b, (dims, ((), ())), preferred_element_type=f32)


HALF = NPTS // 2


def square_place():
    pa = lax.axis_index("pa")
    return 2 * ((pa // 16) % 2) + (pa // 4) % 2


def points_of(x_ref, here, kk, rows):
    return jnp.concatenate([x_ref[(2 * kk) ^ here, rows, :], x_ref[(2 * kk + 1) ^ here, rows, :]], axis=1)


def term_columns(half, x_ref, t_ref, own_ref, term_ref):
    here = square_place()
    acc = None
    for kk in range(2):
        xq = points_of(x_ref, here, kk, pl.ds(half * HALF, HALF))
        v = dot(t_ref[kk], xq, NT)
        own_ref[kk] = v
        w = dot(t_ref[2 + kk], xq, NT)
        acc = v * v - w * w if acc is None else acc + (v * v - w * w)
    term_ref[...] = acc.astype(bf16)


def first_kernel(x_ref, g_mine, g_else, t_ref, own_ref, term_ref):
    here = square_place()
    for kk in range(2):
        xk = points_of(x_ref, here, kk, pl.ds(0, NPTS))
        t_ref[kk] = dot(xk, g_mine[kk]).astype(bf16)
        t_ref[2 + kk] = dot(xk, g_else[kk]).astype(bf16)
    term_columns(0, x_ref, t_ref, own_ref, term_ref)


def second_kernel(x_ref, t_ref, own_ref, term_ref):
    term_columns(1, x_ref, t_ref, own_ref, term_ref)


def bubble_of(term0, term1):
    return ((term0[...].astype(f32) + term1[...].astype(f32)) * 0.25).astype(bf16)


def third_kernel(TW, core_ref, term0, term1, mix_ref, bub_ref):
    bub_ref[...] = bubble_of(term0, term1)

    def step(i, _):
        rows = pl.ds(pl.multiple_of(i * TW, TW), TW)
        mix_ref[rows, :] = dot(core_ref[rows, :], bub_ref[...]).astype(bf16)
        return 0

    lax.fori_loop(0, NPTS // TW, step, 0)


def fourth_kernel(TW, core_ref, mix0, term0, term1, own0, own1, x_ref, out_ref, bub_ref, mix1, tmp_ref):
    here = square_place()
    every = pl.ds(0, NPTS)
    third_kernel(TW, core_ref, term0, term1, mix1, bub_ref)

    def step(i, _):
        rows = pl.ds(pl.multiple_of(i * TW, TW), TW)
        w = dot(jnp.concatenate([mix0[rows, :], mix1[rows, :]], axis=1), core_ref[...])
        for kk in range(2):
            own = jnp.concatenate([own0[kk, rows, :], own1[kk, rows, :]], axis=1)
            source = (own * w).astype(bf16)
            tmp_ref[kk, rows, :] = dot(source, points_of(x_ref, here, kk, every)).astype(bf16)
        return 0

    lax.fori_loop(0, NPTS // TW, step, 0)
    for kk in range(2):
        out_ref[kk] = dot(points_of(x_ref, here, kk, every), tmp_ref[kk], TN).astype(bf16)


VM = pl.BlockSpec(memory_space=pltpu.VMEM)


def call(kernel, n_in, outs, scratch, gflops, limit):
    return pl.pallas_call(
        kernel,
        out_shape=tuple(jax.ShapeDtypeStruct(*o) for o in outs),
        in_specs=[VM] * n_in,
        out_specs=tuple(VM for _ in outs),
        scratch_shapes=[pltpu.VMEM(*o) for o in scratch],
        compiler_params=pltpu.CompilerParams(vmem_limit_bytes=limit << 20),
        cost_estimate=pl.CostEstimate(flops=int(gflops * 1e9), bytes_accessed=2 << 20, transcendentals=0),
    )


T_OUT = ((4, NPTS, NORB), bf16)
OWN_OUT = ((2, NPTS, HALF), f32)
HALF_OUT = ((NPTS, HALF), bf16)


def to_green(rows):
    parts = rows.reshape(64, 2, 2, 4, 128)
    return jnp.transpose(parts, (2, 0, 3, 1, 4)).reshape(2, NORB, NORB)


def local(green_freq, colloc, core):
    ta = lax.axis_index("ta")
    c = ta % 2
    cosine, sine = half_tables()
    table = jnp.where(ta < 2, cosine, sine)
    own_w = lax.dynamic_slice_in_dim(table, c * 64, 64, 1)
    other_w = lax.dynamic_slice_in_dim(table, 64 - c * 64, 64, 1)

    gf = green_freq.reshape(64, 2, 8, NORB)
    mine = lax.dynamic_index_in_dim(gf, c, 1, keepdims=False)
    theirs = lax.dynamic_index_in_dim(gf, 1 - c, 1, keepdims=False)
    arrived = lax.ppermute(theirs, "ta", CORE_SWAP)
    part = jnp.einsum("uw,wrj->urj", own_w, mine.astype(f32), precision=lax.Precision.HIGHEST)
    part += jnp.einsum("uw,wrj->urj", other_w, arrived.astype(f32), precision=lax.Precision.HIGHEST)
    part = part.astype(bf16).reshape(64, 8, 2, 128).swapaxes(1, 2).reshape(64, 16, 128)

    xt = jnp.swapaxes(colloc, 1, 2).reshape(2, 2, 16, 2, 128)
    xt = lax.dynamic_index_in_dim(xt, c, 0, keepdims=False).swapaxes(1, 2).reshape(4, 16, 128)
    xmsg = jnp.broadcast_to(xt.reshape(1, 2, 1, 2, 1, 16, 128), (2, 2, 2, 2, 4, 16, 128)).reshape(64, 16, 128)
    got = lax.all_to_all(jnp.concatenate([part, xmsg], 1), "pa", 0, 0, tiled=True)
    g_own = to_green(got[:, :16])
    xpart = got[:, 16:].reshape(NPTS, 128)

    g_kind = lax.ppermute(g_own, "ta", CHIP_SWAP)
    pieces = [xpart]
    for s in (1, 2, 3):
        pieces.append(lax.ppermute(xpart, ("ta", "pa"), square_pairs(s)))
    x_own = jnp.stack(pieces)
    t, own0, term0 = call(first_kernel, 3, (T_OUT, OWN_OUT, HALF_OUT), (), 1.6, 16)(x_own, g_own, g_kind)
    term0_next = lax.ppermute(term0, "ta", CORE_SWAP)
    own1, term1 = call(second_kernel, 2, (OWN_OUT, HALF_OUT), (), 1.1, 16)(x_own, t)
    term1_next = lax.ppermute(term1, "ta", CORE_SWAP)
    (mix0,) = call(functools.partial(third_kernel, 512), 3, (HALF_OUT,), (HALF_OUT,), 1.1, 8)(core, term0, term0_next)
    (out,) = call(
        functools.partial(fourth_kernel, 512),
        7,
        (((2, NORB, NORB), bf16),),
        (HALF_OUT, HALF_OUT, ((2, NPTS, NORB), bf16)),
        4.6,
        20,
    )(core, mix0, term1, term1_next, own0, own1, x_own)

    msg = out.reshape(2, 64, 4, NORB).swapaxes(0, 1).reshape(64, 8, NORB)
    back = lax.all_to_all(msg, "pa", 0, 0, tiled=True)
    back_next = lax.ppermute(back, "ta", CORE_SWAP)
    first = jnp.where(c == 0, back, back_next)
    second = jnp.where(c == 0, back_next, back)
    both = jnp.concatenate([first, second], 1)
    final = own_w * jnp.where(ta < 2, 2.0, -2.0)
    result = jnp.einsum("uw,urj->wrj", final, both.astype(f32), precision=lax.Precision.HIGHEST)
    return result.astype(bf16).reshape(64, 4, 4, NORB)


def solution(mesh):
    return jax.shard_map(
        local,
        mesh=mesh,
        in_specs=(P("ta", None, "pa", None), P(None, None, "pa"), P()),
        out_specs=P("ta", None, "pa", None),
        check_vma=False,
    )
```

```python
import functools

import jax
import jax.numpy as jnp
from jax import lax
from jax.experimental import pallas as pl
from jax.experimental.pallas import tpu as pltpu
from jax.sharding import PartitionSpec as P


NFREQ = 128
NPTS = 1024
NORB = 256
bf16 = jnp.bfloat16
f32 = jnp.float32

CORE_SWAP = [(0, 1), (1, 0), (2, 3), (3, 2)]
CHIP_SWAP = [(0, 2), (2, 0), (1, 3), (3, 1)]
NT = ((1,), (1,))
TN = ((0,), (0,))


def square_pairs(step):
    def partner(v, core):
        return v ^ 1 if core == 0 else ((v + 1) ^ 1) - 1 & 3

    pairs = []
    for ta in range(4):
        for i in range(64):
            x, y, z = i // 16, (i // 4) % 4, i % 4
            x = partner(x, ta % 2) if step & 2 else x
            y = partner(y, ta % 2) if step & 1 else y
            pairs.append((ta * 64 + i, ta * 64 + x * 16 + y * 4 + z))
    return pairs


def half_tables():
    freq = jnp.arange(NFREQ, dtype=f32)
    times = jnp.arange(NFREQ // 2, dtype=f32)
    phase = jnp.pi * (2.0 * freq[None, :] + 1.0) * (times[:, None] + 0.5) / NFREQ
    scale = 1.0 / jnp.sqrt(f32(NFREQ))
    return jnp.cos(phase) * scale, jnp.sin(phase) * scale


def dot(a, b, dims=((1,), (0,))):
    return lax.dot_general(a, b, (dims, ((), ())), preferred_element_type=f32)


HALF = NPTS // 2


def square_place():
    pa = lax.axis_index("pa")
    return 2 * ((pa // 16) % 2) + (pa // 4) % 2


def points_of(x_ref, here, kk, rows):
    return jnp.concatenate([x_ref[(2 * kk) ^ here, rows, :], x_ref[(2 * kk + 1) ^ here, rows, :]], axis=1)


def term_columns(half, x_ref, t_ref, own_ref, term_ref):
    here = square_place()
    acc = None
    for kk in range(2):
        xq = points_of(x_ref, here, kk, pl.ds(half * HALF, HALF))
        v = dot(t_ref[kk], xq, NT)
        own_ref[kk] = v
        w = dot(t_ref[2 + kk], xq, NT)
        acc = v * v - w * w if acc is None else acc + (v * v - w * w)
    term_ref[...] = acc.astype(bf16)


def first_kernel(x_ref, g_mine, g_else, t_ref, own_ref, term_ref):
    here = square_place()
    for kk in range(2):
        xk = points_of(x_ref, here, kk, pl.ds(0, NPTS))
        t_ref[kk] = dot(xk, g_mine[kk]).astype(bf16)
        t_ref[2 + kk] = dot(xk, g_else[kk]).astype(bf16)
    term_columns(0, x_ref, t_ref, own_ref, term_ref)


def second_kernel(x_ref, t_ref, own_ref, term_ref):
    term_columns(1, x_ref, t_ref, own_ref, term_ref)


def bubble_of(term0, term1):
    return ((term0[...].astype(f32) + term1[...].astype(f32)) * 0.25).astype(bf16)


def third_kernel(TW, core_ref, term0, term1, mix_ref, bub_ref):
    bub_ref[...] = bubble_of(term0, term1)

    def step(i, _):
        rows = pl.ds(pl.multiple_of(i * TW, TW), TW)
        mix_ref[rows, :] = dot(core_ref[rows, :], bub_ref[...]).astype(bf16)
        return 0

    lax.fori_loop(0, NPTS // TW, step, 0)


def fourth_kernel(TW, core_ref, mix0, term0, term1, own0, own1, x_ref, out_ref, bub_ref, mix1, tmp_ref):
    here = square_place()
    every = pl.ds(0, NPTS)
    third_kernel(TW, core_ref, term0, term1, mix1, bub_ref)

    def step(i, _):
        rows = pl.ds(pl.multiple_of(i * TW, TW), TW)
        w = dot(jnp.concatenate([mix0[rows, :], mix1[rows, :]], axis=1), core_ref[...])
        for kk in range(2):
            own = jnp.concatenate([own0[kk, rows, :], own1[kk, rows, :]], axis=1)
            source = (own * w).astype(bf16)
            tmp_ref[kk, rows, :] = dot(source, points_of(x_ref, here, kk, every)).astype(bf16)
        return 0

    lax.fori_loop(0, NPTS // TW, step, 0)
    for kk in range(2):
        out_ref[kk] = dot(points_of(x_ref, here, kk, every), tmp_ref[kk], TN).astype(bf16)


def split(x):
    high = x.astype(bf16)
    return high, (x - high.astype(f32)).astype(bf16)


def one_hot(shape, which):
    r = lax.broadcasted_iota(jnp.int32, shape, 0)
    c = lax.broadcasted_iota(jnp.int32, shape, 1)
    return ((r >> 3) == c if which == 0 else r == (c >> 3)).astype(f32).astype(bf16)


def spread(table, dims):
    r = lax.broadcasted_iota(jnp.int32, (512, 512), 0)
    c = lax.broadcasted_iota(jnp.int32, (512, 512), 1)
    wide = dot(one_hot((512, 64), 0), table, dims).astype(bf16)
    return jnp.where(((r ^ c) & 7) == 0, dot(wide, one_hot((64, 512), 1)), 0.0).astype(bf16)


def rows_of(ref):
    return ref[...].reshape(512, NORB)


def early_kernel(own_ref, other_ref, rows_ref, part_ref, table_ref):
    part_ref[...] = dot(spread(own_ref[...].astype(bf16), ((1,), (0,))), rows_of(rows_ref))
    table_ref[...] = spread(other_ref[...].astype(bf16), ((1,), (0,)))


def message_kernel(part_ref, table_ref, rows_ref, x_ref, out_ref):
    green = part_ref[...] + dot(table_ref[...], rows_of(rows_ref))
    green = green.astype(bf16).reshape(64, 8, NORB)
    out_ref[:, 0:8, :] = green[:, :, 0:128]
    out_ref[:, 8:16, :] = green[:, :, 128:256]
    for i in range(64):
        out_ref[i, 16:32, :] = x_ref[2 * ((i // 16) % 2) + (i // 4) % 2]


def tables_kernel(table_ref, high_ref, low_ref):
    for x, ref in zip(split(table_ref[...]), (high_ref, low_ref)):
        ref[...] = spread(x, ((1,), (1,)))


def back_rows(high_ref, low_ref, rows_ref):
    rows = rows_of(rows_ref)
    return (dot(high_ref[...], rows) + dot(low_ref[...], rows)).reshape(64, 8, NORB)


def own_rows_kernel(high_ref, low_ref, rows_ref, out_ref):
    own = back_rows(high_ref, low_ref, rows_ref)
    for kk in range(2):
        out_ref[:, kk] = own[:, 4 * kk : 4 * kk + 4].astype(bf16)


def result_kernel(high_ref, low_ref, rows_ref, own_ref, out_ref):
    mine = lax.axis_index("ta") % 2
    out_ref[:, pl.ds(2 * mine, 2)] = own_ref[...]
    other = back_rows(high_ref, low_ref, rows_ref)
    for kk in range(2):
        out_ref[:, 2 - 2 * mine + kk] = other[:, 4 * kk : 4 * kk + 4].astype(bf16)


VM = pl.BlockSpec(memory_space=pltpu.VMEM)


def call(kernel, n_in, outs, scratch, gflops, limit):
    return pl.pallas_call(
        kernel,
        out_shape=tuple(jax.ShapeDtypeStruct(*o) for o in outs),
        in_specs=[VM] * n_in,
        out_specs=tuple(VM for _ in outs),
        scratch_shapes=[pltpu.VMEM(*o) for o in scratch],
        compiler_params=pltpu.CompilerParams(vmem_limit_bytes=limit << 20),
        cost_estimate=pl.CostEstimate(flops=int(gflops * 1e9), bytes_accessed=2 << 20, transcendentals=0),
    )


T_OUT = ((4, NPTS, NORB), bf16)
OWN_OUT = ((2, NPTS, HALF), f32)
HALF_OUT = ((NPTS, HALF), bf16)


def to_green(got):
    rows = jnp.concatenate([got[:, 0:8], got[:, 8:16]], axis=2)
    return rows.reshape(64, 2, 4, NORB).swapaxes(0, 1).reshape(2, NORB, NORB)


def local(green_freq, colloc, core):
    ta = lax.axis_index("ta")
    c = ta % 2
    cosine, sine = half_tables()
    table = jnp.where(ta < 2, cosine, sine)
    own_w = lax.dynamic_slice_in_dim(table, c * 64, 64, 1)
    other_w = lax.dynamic_slice_in_dim(table, 64 - c * 64, 64, 1)

    matrix = ((512, 512), bf16)
    gf = green_freq.reshape(64, 2, 2, 4, NORB)
    theirs = lax.dynamic_index_in_dim(gf, 1 - c, 1, keepdims=False).reshape(64, 8, NORB)
    arrived = lax.ppermute(theirs, "ta", CORE_SWAP)
    mine = lax.dynamic_index_in_dim(gf, c, 1, keepdims=False).reshape(64, 8, NORB)
    part, rest = call(early_kernel, 3, (((512, NORB), f32), matrix), (), 1.0, 10)(
        own_w, other_w, mine
    )
    xt = lax.dynamic_slice_in_dim(jnp.swapaxes(colloc, 1, 2), 2 * c, 2, 0)
    xt = jnp.concatenate([xt[0:1, :, :128], xt[0:1, :, 128:], xt[1:2, :, :128], xt[1:2, :, 128:]], 0)
    (msg,) = call(message_kernel, 4, (((64, 32, 128), bf16),), (), 0.4, 8)(part, rest, arrived, xt)
    got = lax.all_to_all(msg, "pa", 0, 0, tiled=True)
    g_own = to_green(got)
    xpart = got[:, 16:].reshape(NPTS, 128)

    g_kind = lax.ppermute(g_own, "ta", CHIP_SWAP)
    pieces = [xpart]
    for s in (1, 2, 3):
        pieces.append(lax.ppermute(xpart, ("ta", "pa"), square_pairs(s)))
    final = own_w * jnp.where(ta < 2, 2.0, -2.0)
    back_high, back_low = call(tables_kernel, 1, (matrix, matrix), (), 0.3, 8)(final)
    x_own = jnp.stack(pieces)
    t, own0, term0 = call(first_kernel, 3, (T_OUT, OWN_OUT, HALF_OUT), (), 1.6, 16)(x_own, g_own, g_kind)
    term0_next = lax.ppermute(term0, "ta", CORE_SWAP)
    own1, term1 = call(second_kernel, 2, (OWN_OUT, HALF_OUT), (), 1.1, 16)(x_own, t)
    term1_next = lax.ppermute(term1, "ta", CORE_SWAP)
    (mix0,) = call(functools.partial(third_kernel, 512), 3, (HALF_OUT,), (HALF_OUT,), 1.1, 8)(core, term0, term0_next)
    (out,) = call(
        functools.partial(fourth_kernel, 512),
        7,
        (((2, NORB, NORB), bf16),),
        (HALF_OUT, HALF_OUT, ((2, NPTS, NORB), bf16)),
        4.6,
        20,
    )(core, mix0, term1, term1_next, own0, own1, x_own)

    msg = out.reshape(2, 64, 4, NORB).swapaxes(0, 1).reshape(64, 8, NORB)
    back = lax.all_to_all(msg, "pa", 0, 0, tiled=True)
    back_next = lax.ppermute(back, "ta", CORE_SWAP)
    (own_rows,) = call(own_rows_kernel, 3, (((64, 2, 4, NORB), bf16),), (), 0.3, 8)(back_high, back_low, back)
    (result,) = call(result_kernel, 4, (((64, 4, 4, NORB), bf16),), (), 0.3, 8)(
        back_high, back_low, back_next, own_rows
    )
    return result


def solution(mesh):
    return jax.shard_map(
        local,
        mesh=mesh,
        in_specs=(P("ta", None, "pa", None), P(None, None, "pa"), P()),
        out_specs=P("ta", None, "pa", None),
        check_vma=False,
    )
```

```python
import jax
import jax.numpy as jnp
from jax import lax
from jax.experimental import pallas as pl
from jax.experimental.pallas import tpu as pltpu
from jax.sharding import PartitionSpec as P


NFREQ = 128
NPTS = 1024
NORB = 256
bf16 = jnp.bfloat16
f32 = jnp.float32

CORE_SWAP = [(0, 1), (1, 0), (2, 3), (3, 2)]
CHIP_SWAP = [(0, 2), (2, 0), (1, 3), (3, 1)]
NT = ((1,), (1,))
TN = ((0,), (0,))


def square_pairs(step):
    def partner(v, core):
        return v ^ 1 if core == 0 else ((v + 1) ^ 1) - 1 & 3

    pairs = []
    for ta in range(4):
        for i in range(64):
            x, y, z = i // 16, (i // 4) % 4, i % 4
            x = partner(x, ta % 2) if step & 2 else x
            y = partner(y, ta % 2) if step & 1 else y
            pairs.append((ta * 64 + i, ta * 64 + x * 16 + y * 4 + z))
    return pairs


def half_tables():
    freq = jnp.arange(NFREQ, dtype=f32)
    times = jnp.arange(NFREQ // 2, dtype=f32)
    phase = jnp.pi * (2.0 * freq[None, :] + 1.0) * (times[:, None] + 0.5) / NFREQ
    scale = 1.0 / jnp.sqrt(f32(NFREQ))
    return jnp.cos(phase) * scale, jnp.sin(phase) * scale


def dot(a, b, dims=((1,), (0,))):
    return lax.dot_general(a, b, (dims, ((), ())), preferred_element_type=f32)


HALF = NPTS // 2
STRIP = 512


def square_place():
    pa = lax.axis_index("pa")
    return 2 * ((pa // 16) % 2) + (pa // 4) % 2


def points_of(x_ref, here, kk, rows):
    return jnp.concatenate([x_ref[(2 * kk) ^ here, rows, :], x_ref[(2 * kk + 1) ^ here, rows, :]], axis=1)


def term_columns(half, x_ref, t_ref, own_ref, term_ref):
    here = square_place()
    acc = None
    for kk in range(2):
        xq = points_of(x_ref, here, kk, pl.ds(half * HALF, HALF))
        v = dot(t_ref[kk], xq, NT)
        own_ref[kk] = v
        w = dot(t_ref[2 + kk], xq, NT)
        acc = v * v - w * w if acc is None else acc + (v * v - w * w)
    term_ref[...] = acc.astype(bf16)


def first_kernel(x_ref, g_mine, g_else, t_ref, own_ref, term_ref):
    here = square_place()
    for kk in range(2):
        xk = points_of(x_ref, here, kk, pl.ds(0, NPTS))
        t_ref[kk] = dot(xk, g_mine[kk]).astype(bf16)
        t_ref[2 + kk] = dot(xk, g_else[kk]).astype(bf16)
    term_columns(0, x_ref, t_ref, own_ref, term_ref)


def second_kernel(x_ref, t_ref, own_ref, term_ref):
    term_columns(1, x_ref, t_ref, own_ref, term_ref)


def bubble_of(term0, term1):
    return ((term0[...].astype(f32) + term1[...].astype(f32)) * 0.25).astype(bf16)


def mixed_columns(core_ref, term0, term1, mix_ref, bub_ref):
    bub_ref[...] = bubble_of(term0, term1)
    mix_ref[...] = dot(core_ref[...], bub_ref[...]).astype(bf16)


def third_kernel(core_ref, term0, term1, mix_ref, bub_ref):
    mixed_columns(core_ref, term0, term1, mix_ref, bub_ref)


def fourth_kernel(core_ref, mix0, term0, term1, own0, own1, x_ref, out_ref, bub_ref, mix1, tmp_ref):
    here = square_place()
    every = pl.ds(0, NPTS)
    mixed_columns(core_ref, term0, term1, mix1, bub_ref)
    for i in range(NPTS // STRIP):
        rows = pl.ds(i * STRIP, STRIP)
        w = dot(jnp.concatenate([mix0[rows, :], mix1[rows, :]], axis=1), core_ref[...])
        for kk in range(2):
            own = jnp.concatenate([own0[kk, rows, :], own1[kk, rows, :]], axis=1)
            source = (own * w).astype(bf16)
            tmp_ref[kk, rows, :] = dot(source, points_of(x_ref, here, kk, every)).astype(bf16)
    for kk in range(2):
        out_ref[kk] = dot(points_of(x_ref, here, kk, every), tmp_ref[kk], TN).astype(bf16)


def one_hot(shape, which):
    r = lax.broadcasted_iota(jnp.int32, shape, 0)
    c = lax.broadcasted_iota(jnp.int32, shape, 1)
    return ((r >> 3) == c if which == 0 else r == (c >> 3)).astype(f32).astype(bf16)


def spread(table, dims):
    r = lax.broadcasted_iota(jnp.int32, (512, 512), 0)
    c = lax.broadcasted_iota(jnp.int32, (512, 512), 1)
    wide = dot(one_hot((512, 64), 0), table, dims).astype(bf16)
    return jnp.where(((r ^ c) & 7) == 0, dot(wide, one_hot((64, 512), 1)), 0.0).astype(bf16)


def rows_of(ref):
    return ref[...].reshape(512, NORB)


def early_kernel(own_ref, other_ref, rows_ref, part_ref, table_ref):
    part_ref[...] = dot(spread(own_ref[...].astype(bf16), ((1,), (0,))), rows_of(rows_ref))
    table_ref[...] = spread(other_ref[...].astype(bf16), ((1,), (0,)))


def message_kernel(part_ref, table_ref, rows_ref, x_ref, out_ref):
    green = part_ref[...] + dot(table_ref[...], rows_of(rows_ref))
    green = green.astype(bf16).reshape(64, 8, NORB)
    out_ref[:, 0:8, :] = green[:, :, 0:128]
    out_ref[:, 8:16, :] = green[:, :, 128:256]
    for i in range(64):
        out_ref[i, 16:32, :] = x_ref[2 * ((i // 16) % 2) + (i // 4) % 2]


def tables_kernel(table_ref, out_ref):
    out_ref[...] = spread(table_ref[...].astype(bf16), ((1,), (1,)))


def back_rows(table_ref, rows_ref):
    return dot(table_ref[...], rows_of(rows_ref)).reshape(64, 8, NORB)


def own_rows_kernel(table_ref, rows_ref, out_ref):
    own = back_rows(table_ref, rows_ref)
    for kk in range(2):
        out_ref[:, kk] = own[:, 4 * kk : 4 * kk + 4].astype(bf16)


def result_kernel(table_ref, rows_ref, own_ref, out_ref):
    mine = lax.axis_index("ta") % 2
    out_ref[:, pl.ds(2 * mine, 2)] = own_ref[...]
    other = back_rows(table_ref, rows_ref)
    for kk in range(2):
        out_ref[:, 2 - 2 * mine + kk] = other[:, 4 * kk : 4 * kk + 4].astype(bf16)


VM = pl.BlockSpec(memory_space=pltpu.VMEM)


def call(kernel, n_in, outs, scratch, gflops, limit):
    return pl.pallas_call(
        kernel,
        out_shape=tuple(jax.ShapeDtypeStruct(*o) for o in outs),
        in_specs=[VM] * n_in,
        out_specs=tuple(VM for _ in outs),
        scratch_shapes=[pltpu.VMEM(*o) for o in scratch],
        compiler_params=pltpu.CompilerParams(vmem_limit_bytes=limit << 20),
        cost_estimate=pl.CostEstimate(flops=int(gflops * 1e9), bytes_accessed=2 << 20, transcendentals=0),
    )


T_OUT = ((4, NPTS, NORB), bf16)
OWN_OUT = ((2, NPTS, HALF), f32)
HALF_OUT = ((NPTS, HALF), bf16)


def to_green(got):
    rows = jnp.concatenate([got[:, 0:8], got[:, 8:16]], axis=2)
    return rows.reshape(64, 2, 4, NORB).swapaxes(0, 1).reshape(2, NORB, NORB)


def local(green_freq, colloc, core):
    ta = lax.axis_index("ta")
    c = ta % 2
    cosine, sine = half_tables()
    table = jnp.where(ta < 2, cosine, sine)
    own_w = lax.dynamic_slice_in_dim(table, c * 64, 64, 1)
    other_w = lax.dynamic_slice_in_dim(table, 64 - c * 64, 64, 1)

    matrix = ((512, 512), bf16)
    gf = green_freq.reshape(64, 2, 2, 4, NORB)
    theirs = lax.dynamic_index_in_dim(gf, 1 - c, 1, keepdims=False).reshape(64, 8, NORB)
    arrived = lax.ppermute(theirs, "ta", CORE_SWAP)
    mine = lax.dynamic_index_in_dim(gf, c, 1, keepdims=False).reshape(64, 8, NORB)
    part, rest = call(early_kernel, 3, (((512, NORB), f32), matrix), (), 1.0, 10)(
        own_w, other_w, mine
    )
    xt = lax.dynamic_slice_in_dim(jnp.swapaxes(colloc, 1, 2), 2 * c, 2, 0)
    xt = jnp.concatenate([xt[0:1, :, :128], xt[0:1, :, 128:], xt[1:2, :, :128], xt[1:2, :, 128:]], 0)
    (msg,) = call(message_kernel, 4, (((64, 32, 128), bf16),), (), 0.4, 8)(part, rest, arrived, xt)
    got = lax.all_to_all(msg, "pa", 0, 0, tiled=True)
    g_own = to_green(got)
    xpart = got[:, 16:].reshape(NPTS, 128)

    g_kind = lax.ppermute(g_own, "ta", CHIP_SWAP)
    pieces = [xpart]
    for s in (1, 2, 3):
        pieces.append(lax.ppermute(xpart, ("ta", "pa"), square_pairs(s)))
    final = own_w * jnp.where(ta < 2, 2.0, -2.0)
    (back_table,) = call(tables_kernel, 1, (matrix,), (), 0.3, 8)(final)
    x_own = jnp.stack(pieces)
    t, own0, term0 = call(first_kernel, 3, (T_OUT, OWN_OUT, HALF_OUT), (), 1.6, 16)(x_own, g_own, g_kind)
    term0_next = lax.ppermute(term0, "ta", CORE_SWAP)
    own1, term1 = call(second_kernel, 2, (OWN_OUT, HALF_OUT), (), 1.1, 16)(x_own, t)
    term1_next = lax.ppermute(term1, "ta", CORE_SWAP)
    (mix0,) = call(third_kernel, 3, (HALF_OUT,), (HALF_OUT,), 1.1, 8)(
        core, term0, term0_next
    )
    (out,) = call(
        fourth_kernel,
        7,
        (((2, NORB, NORB), bf16),),
        (HALF_OUT, HALF_OUT, ((2, NPTS, NORB), bf16)),
        4.6,
        20,
    )(core, mix0, term1, term1_next, own0, own1, x_own)

    msg = out.reshape(2, 64, 4, NORB).swapaxes(0, 1).reshape(64, 8, NORB)
    back = lax.all_to_all(msg, "pa", 0, 0, tiled=True)
    back_next = lax.ppermute(back, "ta", CORE_SWAP)
    (own_rows,) = call(own_rows_kernel, 2, (((64, 2, 4, NORB), bf16),), (), 0.3, 8)(back_table, back)
    (result,) = call(result_kernel, 3, (((64, 4, 4, NORB), bf16),), (), 0.3, 8)(
        back_table, back_next, own_rows
    )
    return result


def solution(mesh):
    return jax.shard_map(
        local,
        mesh=mesh,
        in_specs=(P("ta", None, "pa", None), P(None, None, "pa"), P()),
        out_specs=P("ta", None, "pa", None),
        check_vma=False,
    )
```

```python
import jax
import jax.numpy as jnp
from jax import lax
from jax.experimental import pallas as pl
from jax.experimental.pallas import tpu as pltpu
from jax.sharding import PartitionSpec as P


NFREQ = 128
NPTS = 1024
NORB = 256
bf16 = jnp.bfloat16
f32 = jnp.float32

CORE_SWAP = [(0, 1), (1, 0), (2, 3), (3, 2)]
CHIP_SWAP = [(0, 2), (2, 0), (1, 3), (3, 1)]
NT = ((1,), (1,))
TN = ((0,), (0,))


def square_pairs(step):
    def partner(v, core):
        return v ^ 1 if core == 0 else ((v + 1) ^ 1) - 1 & 3

    pairs = []
    for ta in range(4):
        for i in range(64):
            x, y, z = i // 16, (i // 4) % 4, i % 4
            x = partner(x, ta % 2) if step & 2 else x
            y = partner(y, ta % 2) if step & 1 else y
            pairs.append((ta * 64 + i, ta * 64 + x * 16 + y * 4 + z))
    return pairs


def half_tables():
    freq = jnp.arange(NFREQ, dtype=f32)
    times = jnp.arange(NFREQ // 2, dtype=f32)
    phase = jnp.pi * (2.0 * freq[None, :] + 1.0) * (times[:, None] + 0.5) / NFREQ
    scale = 1.0 / jnp.sqrt(f32(NFREQ))
    return jnp.cos(phase) * scale, jnp.sin(phase) * scale


def dot(a, b, dims=((1,), (0,))):
    return lax.dot_general(a, b, (dims, ((), ())), preferred_element_type=f32)


HALF = NPTS // 2
STRIP = 512


def square_place():
    pa = lax.axis_index("pa")
    return 2 * ((pa // 16) % 2) + (pa // 4) % 2


def points_of(x_ref, here, kk, rows):
    return jnp.concatenate([x_ref[(2 * kk) ^ here, rows, :], x_ref[(2 * kk + 1) ^ here, rows, :]], axis=1)


def term_columns(half, x_ref, t_ref, own_ref, term_ref):
    here = square_place()
    acc = None
    for kk in range(2):
        xq = points_of(x_ref, here, kk, pl.ds(half * HALF, HALF))
        v = dot(t_ref[kk], xq, NT)
        own_ref[kk] = v
        w = dot(t_ref[2 + kk], xq, NT)
        acc = v * v - w * w if acc is None else acc + (v * v - w * w)
    term_ref[...] = acc.astype(bf16)


def first_kernel(x_ref, g_mine, g_else, t_ref, own_ref, term_ref):
    here = square_place()
    for kk in range(2):
        xk = points_of(x_ref, here, kk, pl.ds(0, NPTS))
        t_ref[kk] = dot(xk, g_mine[kk]).astype(bf16)
        t_ref[2 + kk] = dot(xk, g_else[kk]).astype(bf16)
    term_columns(0, x_ref, t_ref, own_ref, term_ref)


def second_kernel(x_ref, t_ref, own_ref, term_ref):
    term_columns(1, x_ref, t_ref, own_ref, term_ref)


def bubble_of(term0, term1):
    return ((term0[...].astype(f32) + term1[...].astype(f32)) * 0.25).astype(bf16)


def mixed_columns(core_ref, term0, term1, mix_ref, bub_ref):
    bub_ref[...] = bubble_of(term0, term1)
    mix_ref[...] = dot(core_ref[...], bub_ref[...]).astype(bf16)


def third_kernel(core_ref, term0, term1, mix_ref, bub_ref):
    mixed_columns(core_ref, term0, term1, mix_ref, bub_ref)


def fourth_kernel(core_ref, mix0, term0, term1, own0, own1, x_ref, out_ref, bub_ref, mix1, tmp_ref):
    here = square_place()
    every = pl.ds(0, NPTS)
    mixed_columns(core_ref, term0, term1, mix1, bub_ref)
    for i in range(NPTS // STRIP):
        rows = pl.ds(i * STRIP, STRIP)
        w = dot(jnp.concatenate([mix0[rows, :], mix1[rows, :]], axis=1), core_ref[...])
        for kk in range(2):
            own = jnp.concatenate([own0[kk, rows, :], own1[kk, rows, :]], axis=1)
            source = (own * w).astype(bf16)
            tmp_ref[kk, rows, :] = dot(source, points_of(x_ref, here, kk, every)).astype(bf16)
    rows = [dot(points_of(x_ref, here, kk, every), tmp_ref[kk], TN).reshape(64, 4, NORB) for kk in range(2)]
    out_ref[...] = jnp.concatenate(rows, axis=1).astype(bf16)


def one_hot(shape, which):
    r = lax.broadcasted_iota(jnp.int32, shape, 0)
    c = lax.broadcasted_iota(jnp.int32, shape, 1)
    return ((r >> 3) == c if which == 0 else r == (c >> 3)).astype(f32).astype(bf16)


def spread(table, dims):
    r = lax.broadcasted_iota(jnp.int32, (512, 512), 0)
    c = lax.broadcasted_iota(jnp.int32, (512, 512), 1)
    wide = dot(one_hot((512, 64), 0), table, dims).astype(bf16)
    return jnp.where(((r ^ c) & 7) == 0, dot(wide, one_hot((64, 512), 1)), 0.0).astype(bf16)


def rows_of(ref):
    return ref[...].reshape(512, NORB)


def early_kernel(own_ref, other_ref, rows_ref, part_ref, table_ref):
    part_ref[...] = dot(spread(own_ref[...].astype(bf16), ((1,), (0,))), rows_of(rows_ref))
    table_ref[...] = spread(other_ref[...].astype(bf16), ((1,), (0,)))


def message_kernel(part_ref, table_ref, rows_ref, x_ref, out_ref):
    green = part_ref[...] + dot(table_ref[...], rows_of(rows_ref))
    green = green.astype(bf16).reshape(64, 8, NORB)
    out_ref[:, 0:8, :] = green[:, :, 0:128]
    out_ref[:, 8:16, :] = green[:, :, 128:256]
    for i in range(64):
        out_ref[i, 16:32, :] = x_ref[2 * ((i // 16) % 2) + (i // 4) % 2]


def tables_kernel(table_ref, out_ref):
    out_ref[...] = spread(table_ref[...].astype(bf16), ((1,), (1,)))


def back_rows(table_ref, rows_ref):
    return dot(table_ref[...], rows_of(rows_ref)).reshape(64, 8, NORB)


def own_rows_kernel(table_ref, rows_ref, out_ref):
    own = back_rows(table_ref, rows_ref)
    for kk in range(2):
        out_ref[:, kk] = own[:, 4 * kk : 4 * kk + 4].astype(bf16)


def result_kernel(table_ref, rows_ref, own_ref, out_ref):
    mine = lax.axis_index("ta") % 2
    out_ref[:, pl.ds(2 * mine, 2)] = own_ref[...]
    other = back_rows(table_ref, rows_ref)
    for kk in range(2):
        out_ref[:, 2 - 2 * mine + kk] = other[:, 4 * kk : 4 * kk + 4].astype(bf16)


VM = pl.BlockSpec(memory_space=pltpu.VMEM)


def call(kernel, n_in, outs, scratch, gflops, limit):
    return pl.pallas_call(
        kernel,
        out_shape=tuple(jax.ShapeDtypeStruct(*o) for o in outs),
        in_specs=[VM] * n_in,
        out_specs=tuple(VM for _ in outs),
        scratch_shapes=[pltpu.VMEM(*o) for o in scratch],
        compiler_params=pltpu.CompilerParams(vmem_limit_bytes=limit << 20),
        cost_estimate=pl.CostEstimate(flops=int(gflops * 1e9), bytes_accessed=2 << 20, transcendentals=0),
    )


T_OUT = ((4, NPTS, NORB), bf16)
OWN_OUT = ((2, NPTS, HALF), f32)
HALF_OUT = ((NPTS, HALF), bf16)


def to_green(got):
    rows = jnp.concatenate([got[:, 0:8], got[:, 8:16]], axis=2)
    return rows.reshape(64, 2, 4, NORB).swapaxes(0, 1).reshape(2, NORB, NORB)


def local(green_freq, colloc, core):
    ta = lax.axis_index("ta")
    c = ta % 2
    cosine, sine = half_tables()
    table = jnp.where(ta < 2, cosine, sine)
    own_w = lax.dynamic_slice_in_dim(table, c * 64, 64, 1)
    other_w = lax.dynamic_slice_in_dim(table, 64 - c * 64, 64, 1)

    matrix = ((512, 512), bf16)
    gf = green_freq.reshape(64, 2, 2, 4, NORB)
    theirs = lax.dynamic_index_in_dim(gf, 1 - c, 1, keepdims=False).reshape(64, 8, NORB)
    arrived = lax.ppermute(theirs, "ta", CORE_SWAP)
    mine = lax.dynamic_index_in_dim(gf, c, 1, keepdims=False).reshape(64, 8, NORB)
    part, rest = call(early_kernel, 3, (((512, NORB), f32), matrix), (), 1.0, 10)(
        own_w, other_w, mine
    )
    xt = lax.dynamic_slice_in_dim(jnp.swapaxes(colloc, 1, 2), 2 * c, 2, 0)
    xt = jnp.concatenate([xt[0:1, :, :128], xt[0:1, :, 128:], xt[1:2, :, :128], xt[1:2, :, 128:]], 0)
    (msg,) = call(message_kernel, 4, (((64, 32, 128), bf16),), (), 0.4, 8)(part, rest, arrived, xt)
    got = lax.all_to_all(msg, "pa", 0, 0, tiled=True)
    g_own = to_green(got)
    xpart = got[:, 16:].reshape(NPTS, 128)

    g_kind = to_green(lax.ppermute(got[:, :16], "ta", CHIP_SWAP))
    pieces = [xpart]
    for s in (1, 2, 3):
        pieces.append(lax.ppermute(xpart, ("ta", "pa"), square_pairs(s)))
    final = own_w * jnp.where(ta < 2, 2.0, -2.0)
    (back_table,) = call(tables_kernel, 1, (matrix,), (), 0.3, 8)(final)
    x_own = jnp.stack(pieces)
    t, own0, term0 = call(first_kernel, 3, (T_OUT, OWN_OUT, HALF_OUT), (), 1.6, 16)(x_own, g_own, g_kind)
    term0_next = lax.ppermute(term0, "ta", CORE_SWAP)
    own1, term1 = call(second_kernel, 2, (OWN_OUT, HALF_OUT), (), 1.1, 16)(x_own, t)
    term1_next = lax.ppermute(term1, "ta", CORE_SWAP)
    (mix0,) = call(third_kernel, 3, (HALF_OUT,), (HALF_OUT,), 1.1, 8)(
        core, term0, term0_next
    )
    (out,) = call(
        fourth_kernel,
        7,
        (((64, 8, NORB), bf16),),
        (HALF_OUT, HALF_OUT, ((2, NPTS, NORB), bf16)),
        4.6,
        20,
    )(core, mix0, term1, term1_next, own0, own1, x_own)

    back = lax.all_to_all(out, "pa", 0, 0, tiled=True)
    back_next = lax.ppermute(back, "ta", CORE_SWAP)
    (own_rows,) = call(own_rows_kernel, 2, (((64, 2, 4, NORB), bf16),), (), 0.3, 8)(back_table, back)
    (result,) = call(result_kernel, 3, (((64, 4, 4, NORB), bf16),), (), 0.3, 8)(
        back_table, back_next, own_rows
    )
    return result


def solution(mesh):
    return jax.shard_map(
        local,
        mesh=mesh,
        in_specs=(P("ta", None, "pa", None), P(None, None, "pa"), P()),
        out_specs=P("ta", None, "pa", None),
        check_vma=False,
    )
```

```python
import jax
import jax.numpy as jnp
from jax import lax
from jax.experimental import pallas as pl
from jax.experimental.pallas import tpu as pltpu
from jax.sharding import PartitionSpec as P


NFREQ = 128
NPTS = 1024
NORB = 256
bf16 = jnp.bfloat16
f32 = jnp.float32

CORE_SWAP = [(0, 1), (1, 0), (2, 3), (3, 2)]
CHIP_SWAP = [(0, 2), (2, 0), (1, 3), (3, 1)]
NT = ((1,), (1,))
TN = ((0,), (0,))


def square_pairs(step):
    def partner(v, core):
        return v ^ 1 if core == 0 else ((v + 1) ^ 1) - 1 & 3

    pairs = []
    for ta in range(4):
        for i in range(64):
            x, y, z = i // 16, (i // 4) % 4, i % 4
            x = partner(x, ta % 2) if step & 2 else x
            y = partner(y, ta % 2) if step & 1 else y
            pairs.append((ta * 64 + i, ta * 64 + x * 16 + y * 4 + z))
    return pairs


def half_tables():
    freq = jnp.arange(NFREQ, dtype=f32)
    times = jnp.arange(NFREQ // 2, dtype=f32)
    phase = jnp.pi * (2.0 * freq[None, :] + 1.0) * (times[:, None] + 0.5) / NFREQ
    scale = 1.0 / jnp.sqrt(f32(NFREQ))
    return jnp.cos(phase) * scale, jnp.sin(phase) * scale


def dot(a, b, dims=((1,), (0,))):
    return lax.dot_general(a, b, (dims, ((), ())), preferred_element_type=f32)


HALF = NPTS // 2
STRIP = 512


def square_place():
    pa = lax.axis_index("pa")
    return 2 * ((pa // 16) % 2) + (pa // 4) % 2


def points_of(x_ref, here, kk, rows):
    return jnp.concatenate([x_ref[(2 * kk) ^ here, rows, :], x_ref[(2 * kk + 1) ^ here, rows, :]], axis=1)


def term_columns(half, x_ref, t_ref, own_ref, term_ref):
    here = square_place()
    acc = None
    for kk in range(2):
        xq = points_of(x_ref, here, kk, pl.ds(half * HALF, HALF))
        v = dot(t_ref[kk], xq, NT)
        own_ref[kk] = v.astype(bf16)
        w = dot(t_ref[2 + kk], xq, NT)
        acc = v * v - w * w if acc is None else acc + (v * v - w * w)
    term_ref[...] = acc.astype(bf16)


def first_kernel(x_ref, g_mine, g_else, t_ref, own_ref, term_ref):
    here = square_place()
    for kk in range(2):
        xk = points_of(x_ref, here, kk, pl.ds(0, NPTS))
        t_ref[kk] = dot(xk, g_mine[kk]).astype(bf16)
        t_ref[2 + kk] = dot(xk, g_else[kk]).astype(bf16)
    term_columns(0, x_ref, t_ref, own_ref, term_ref)


def second_kernel(x_ref, t_ref, own_ref, term_ref):
    term_columns(1, x_ref, t_ref, own_ref, term_ref)


def bubble_of(term0, term1):
    return ((term0[...].astype(f32) + term1[...].astype(f32)) * 0.25).astype(bf16)


def mixed_columns(core_ref, term0, term1, mix_ref, bub_ref):
    bub_ref[...] = bubble_of(term0, term1)
    mix_ref[...] = dot(core_ref[...], bub_ref[...]).astype(bf16)


def third_kernel(core_ref, term0, term1, mix_ref, bub_ref):
    mixed_columns(core_ref, term0, term1, mix_ref, bub_ref)


def fourth_kernel(core_ref, mix0, term0, term1, own0, own1, x_ref, out_ref, bub_ref, mix1, tmp_ref):
    here = square_place()
    every = pl.ds(0, NPTS)
    mixed_columns(core_ref, term0, term1, mix1, bub_ref)
    for i in range(NPTS // STRIP):
        rows = pl.ds(i * STRIP, STRIP)
        w = dot(jnp.concatenate([mix0[rows, :], mix1[rows, :]], axis=1), core_ref[...])
        for kk in range(2):
            own = jnp.concatenate([own0[kk, rows, :], own1[kk, rows, :]], axis=1)
            source = (own.astype(f32) * w).astype(bf16)
            tmp_ref[kk, rows, :] = dot(source, points_of(x_ref, here, kk, every)).astype(bf16)
    rows = [dot(points_of(x_ref, here, kk, every), tmp_ref[kk], TN).reshape(64, 4, NORB) for kk in range(2)]
    out_ref[...] = jnp.concatenate(rows, axis=1).astype(bf16)


def one_hot(shape, which):
    r = lax.broadcasted_iota(jnp.int32, shape, 0)
    c = lax.broadcasted_iota(jnp.int32, shape, 1)
    return ((r >> 3) == c if which == 0 else r == (c >> 3)).astype(f32).astype(bf16)


def spread(table, dims):
    r = lax.broadcasted_iota(jnp.int32, (512, 512), 0)
    c = lax.broadcasted_iota(jnp.int32, (512, 512), 1)
    wide = dot(one_hot((512, 64), 0), table, dims).astype(bf16)
    return jnp.where(((r ^ c) & 7) == 0, dot(wide, one_hot((64, 512), 1)), 0.0).astype(bf16)


def rows_of(ref):
    return ref[...].reshape(512, NORB)


def early_kernel(own_ref, other_ref, rows_ref, part_ref, table_ref):
    part_ref[...] = dot(spread(own_ref[...].astype(bf16), ((1,), (0,))), rows_of(rows_ref))
    table_ref[...] = spread(other_ref[...].astype(bf16), ((1,), (0,)))


def message_kernel(part_ref, table_ref, rows_ref, x_ref, out_ref):
    green = part_ref[...] + dot(table_ref[...], rows_of(rows_ref))
    green = green.astype(bf16).reshape(64, 8, NORB)
    out_ref[:, 0:8, :] = green[:, :, 0:128]
    out_ref[:, 8:16, :] = green[:, :, 128:256]
    for i in range(64):
        out_ref[i, 16:32, :] = x_ref[2 * ((i // 16) % 2) + (i // 4) % 2]


def tables_kernel(table_ref, out_ref):
    out_ref[...] = spread(table_ref[...].astype(bf16), ((1,), (1,)))


def back_rows(table_ref, rows_ref):
    return dot(table_ref[...], rows_of(rows_ref)).reshape(64, 8, NORB)


def own_rows_kernel(table_ref, rows_ref, out_ref):
    own = back_rows(table_ref, rows_ref)
    for kk in range(2):
        out_ref[:, kk] = own[:, 4 * kk : 4 * kk + 4].astype(bf16)


def result_kernel(table_ref, rows_ref, own_ref, out_ref):
    mine = lax.axis_index("ta") % 2
    out_ref[:, pl.ds(2 * mine, 2)] = own_ref[...]
    other = back_rows(table_ref, rows_ref)
    for kk in range(2):
        out_ref[:, 2 - 2 * mine + kk] = other[:, 4 * kk : 4 * kk + 4].astype(bf16)


VM = pl.BlockSpec(memory_space=pltpu.VMEM)


def call(kernel, n_in, outs, scratch, gflops, limit):
    return pl.pallas_call(
        kernel,
        out_shape=tuple(jax.ShapeDtypeStruct(*o) for o in outs),
        in_specs=[VM] * n_in,
        out_specs=tuple(VM for _ in outs),
        scratch_shapes=[pltpu.VMEM(*o) for o in scratch],
        compiler_params=pltpu.CompilerParams(vmem_limit_bytes=limit << 20),
        cost_estimate=pl.CostEstimate(flops=int(gflops * 1e9), bytes_accessed=2 << 20, transcendentals=0),
    )


T_OUT = ((4, NPTS, NORB), bf16)
OWN_OUT = ((2, NPTS, HALF), bf16)
HALF_OUT = ((NPTS, HALF), bf16)


def to_green(got):
    rows = jnp.concatenate([got[:, 0:8], got[:, 8:16]], axis=2)
    return rows.reshape(64, 2, 4, NORB).swapaxes(0, 1).reshape(2, NORB, NORB)


def local(green_freq, colloc, core):
    ta = lax.axis_index("ta")
    c = ta % 2
    cosine, sine = half_tables()
    table = jnp.where(ta < 2, cosine, sine)
    own_w = lax.dynamic_slice_in_dim(table, c * 64, 64, 1)
    other_w = lax.dynamic_slice_in_dim(table, 64 - c * 64, 64, 1)

    matrix = ((512, 512), bf16)
    gf = green_freq.reshape(64, 2, 2, 4, NORB)
    theirs = lax.dynamic_index_in_dim(gf, 1 - c, 1, keepdims=False).reshape(64, 8, NORB)
    arrived = lax.ppermute(theirs, "ta", CORE_SWAP)
    mine = lax.dynamic_index_in_dim(gf, c, 1, keepdims=False).reshape(64, 8, NORB)
    part, rest = call(early_kernel, 3, (((512, NORB), f32), matrix), (), 1.0, 10)(
        own_w, other_w, mine
    )
    xt = lax.dynamic_slice_in_dim(jnp.swapaxes(colloc, 1, 2), 2 * c, 2, 0)
    xt = jnp.concatenate([xt[0:1, :, :128], xt[0:1, :, 128:], xt[1:2, :, :128], xt[1:2, :, 128:]], 0)
    (msg,) = call(message_kernel, 4, (((64, 32, 128), bf16),), (), 0.4, 8)(part, rest, arrived, xt)
    got = lax.all_to_all(msg, "pa", 0, 0, tiled=True)
    g_own = to_green(got)
    xpart = got[:, 16:].reshape(NPTS, 128)

    g_kind = to_green(lax.ppermute(got[:, :16], "ta", CHIP_SWAP))
    pieces = [xpart]
    for s in (1, 2, 3):
        pieces.append(lax.ppermute(xpart, ("ta", "pa"), square_pairs(s)))
    final = own_w * jnp.where(ta < 2, 2.0, -2.0)
    (back_table,) = call(tables_kernel, 1, (matrix,), (), 0.3, 8)(final)
    x_own = jnp.stack(pieces)
    t, own0, term0 = call(first_kernel, 3, (T_OUT, OWN_OUT, HALF_OUT), (), 1.6, 16)(x_own, g_own, g_kind)
    term0_next = lax.ppermute(term0, "ta", CORE_SWAP)
    own1, term1 = call(second_kernel, 2, (OWN_OUT, HALF_OUT), (), 1.1, 16)(x_own, t)
    term1_next = lax.ppermute(term1, "ta", CORE_SWAP)
    (mix0,) = call(third_kernel, 3, (HALF_OUT,), (HALF_OUT,), 1.1, 8)(
        core, term0, term0_next
    )
    (out,) = call(
        fourth_kernel,
        7,
        (((64, 8, NORB), bf16),),
        (HALF_OUT, HALF_OUT, ((2, NPTS, NORB), bf16)),
        4.6,
        20,
    )(core, mix0, term1, term1_next, own0, own1, x_own)

    back = lax.all_to_all(out, "pa", 0, 0, tiled=True)
    back_next = lax.ppermute(back, "ta", CORE_SWAP)
    (own_rows,) = call(own_rows_kernel, 2, (((64, 2, 4, NORB), bf16),), (), 0.3, 8)(back_table, back)
    (result,) = call(result_kernel, 3, (((64, 4, 4, NORB), bf16),), (), 0.3, 8)(
        back_table, back_next, own_rows
    )
    return result


def solution(mesh):
    return jax.shard_map(
        local,
        mesh=mesh,
        in_specs=(P("ta", None, "pa", None), P(None, None, "pa"), P()),
        out_specs=P("ta", None, "pa", None),
        check_vma=False,
    )
```
